32 devices in a mesh: parts: 2 (over x), cluster: 16 (over z, y, core).
Axes of the slice: x: 2, y: 2, z: 4, core: 2. Of those that a mesh axis runs over, the one named last changes fastest.
Arguments:
- queries: float32 [4096, 1024], P(('parts', 'cluster')), parts along dimension 0, may hold values from -1 to 1
- passages: float32 [64, 128, 1024], P(('parts', 'cluster')), parts along dimension 0, may hold values from -6 to 6
- first_blocks: int32 [4096, 4], P(('parts', 'cluster')), parts along dimension 0, may hold values from 0 to 31, all different within a row; in each aligned block of 128 rows (0 to 127, 128 to 255, ...) at most 24 rows name the same one
- followup_blocks: int32 [4096, 4], P(('parts', 'cluster')), parts along dimension 0, may hold values from 0 to 31, all different within a row; in each aligned block of 128 rows (0 to 127, 128 to 255, ...) at most 24 rows name the same one
Outputs:
- expanded: float32 [4096, 1024], P(('parts', 'cluster')), parts along dimension 0
- second_scores: float32 [4096, 4, 128], P(('parts', 'cluster')), parts along dimension 0
The draws below stay inside these ranges and needn't reach their ends.
There are 2 independent parts, one for each index of `parts`. The reference program is written for one: setup_inputs(seed, part) draws one part's arguments, and reference() takes and returns one part's arrays. A program takes and returns all parts, laid end to end along the dimension named above; each array names one. Nothing has to cross between parts.
Inputs may be any that keep to these rules, and one draw needn't show every extreme that they name: `first_blocks`: each row names 4 different blocks; among the queries of one device no block is named more than 24 times, and some block is named exactly 24 times. `followup_blocks`: each row names 4 different blocks; among the queries of one device no block is named more than 24 times, and some block is named exactly 24 times.
All inputs are finite; a program needn't handle non-finite values.
Results may differ from the reference program's by a relative error of at most 0.00014.
Values sent between devices are 32-bit elements; how exact they have to be, the bound alone decides.
No kernel may reach another device: no remote copies, remote signals or barrier semaphores. Data moves between devices by JAX's collectives and lax.ppermute only.
A program may use at most 128 MiB of HBM per device.

```python
import math
from functools import partial
import jax
import jax.numpy as jnp
import numpy as np
from jax import lax

E = 1024
ROWS = 128
KB = 4
Q_DEV = 128
NBLK = 32
QUERIES = 2048
CAP = 24


def draw_queries(key, part):
    bound = float((E + 160) // E)
    base = jax.random.normal(jax.random.fold_in(key, 7002), (QUERIES, E), jnp.float32) * E ** (-0.5)
    return jnp.clip(base, -bound, bound)


def draw_passages(key, part):
    noise = jax.random.normal(jax.random.fold_in(key, 7005), (NBLK, ROWS, E), jnp.float32)
    values = noise
    return jnp.clip(values, -6.0, 6.0)


def shared_out(own_key, own, number, rows, count, top, most, slope):
    order = jax.random.permutation(own_key, count)
    crowded, usual = shares(count, rows * top, most, slope, True), shares(count, rows * top, most, slope, False)
    places = jnp.arange(count)

    def named(sizes, offset_by):
        used = int((sizes > 0).sum())
        fixed = max(1, used // 4)
        moved = fixed + (places - fixed + offset_by * (used - fixed)) % max(1, count - fixed)
        return jnp.zeros((count,), jnp.int32).at[order[jnp.where(places < fixed, places, moved)]].set(jnp.asarray(sizes, jnp.int32))

    sizes = jnp.where(number % 4 == 0, named(crowded, number // 4), named(usual, number - number // 4 - 1))
    mixed = jax.random.permutation(jax.random.fold_in(own, 3), count)
    donor, receiver = mixed[0:count // 2 * 2:2], mixed[1:count // 2 * 2:2]
    margin = jnp.minimum(sizes[donor] - 1, most - sizes[receiver]) // 2
    margin = jnp.where((donor == order[0]) | (receiver == order[0]) | (sizes[receiver] == 0), 0, jnp.maximum(margin, 0))
    moved = jax.random.randint(jax.random.fold_in(own, 4), (count // 2,), 0, 1 << 20) % (margin + 1)
    sizes = sizes.at[donor].add(-moved).at[receiver].add(moved)
    members = jnp.searchsorted(jnp.cumsum(sizes), jnp.arange(rows * top), side="right").astype(jnp.int32)
    grid = members.reshape(top, rows).T
    grid = grid[jax.random.permutation(jax.random.fold_in(own, 1), rows)]
    offset_by = jax.random.randint(jax.random.fold_in(own, 2), (rows, 1), 0, top)
    return jnp.take_along_axis(grid, (jnp.arange(top)[None, :] + offset_by) % top, axis=1)


def shares(number_of, total, reach, slope, full):
    loads = [(1 << 20) // math.isqrt(rank ** slope) + 1 for rank in range(1, number_of + 1)]
    largest = reach if full else min(reach, max(-(-total // number_of), total * loads[0] // sum(loads)))
    least = 1 if total - largest >= number_of - 1 else 0
    holding, spare = [largest] + [least] * (number_of - 1), total - largest - least * (number_of - 1)
    while spare > 0:
        free = [i for i in range(1, number_of) if holding[i] < largest] or [i for i in range(1, number_of) if holding[i] < reach]
        pool, budget = sum([loads[i] for i in free]), spare
        for i in free:
            more = min(reach - holding[i], max(1, budget * loads[i] // pool), spare)
            holding[i] = holding[i] + more
            spare = spare - more
    return np.array(holding)


def setup_inputs(seed: int = 0, part: int = 0) -> dict:
    key_list = jax.random.split(jax.random.key(seed), 5)
    own_keys = jax.random.split(jax.random.fold_in(key_list[4], part), 5)
    queries = draw_queries(jax.random.fold_in(jax.random.fold_in(key_list[4], part), 71), part)
    passages = draw_passages(jax.random.fold_in(jax.random.fold_in(key_list[4], part), 71), part)
    first_blocks_keys = jax.random.split(jax.random.fold_in(own_keys[2], 1), QUERIES // Q_DEV)
    first_blocks_turns = jax.random.permutation(jax.random.fold_in(own_keys[2], 3), QUERIES // Q_DEV)
    first_blocks = jax.vmap(lambda own, number: shared_out(jax.random.fold_in(own_keys[2], 2), own, number, Q_DEV, NBLK, KB, CAP, 2))(first_blocks_keys, first_blocks_turns).reshape((QUERIES, KB))
    followup_blocks_keys = jax.random.split(jax.random.fold_in(own_keys[3], 1), QUERIES // Q_DEV)
    followup_blocks_turns = jax.random.permutation(jax.random.fold_in(own_keys[3], 3), QUERIES // Q_DEV)
    followup_blocks = jax.vmap(lambda own, number: shared_out(jax.random.fold_in(own_keys[3], 2), own, number, Q_DEV, NBLK, KB, CAP, 2))(followup_blocks_keys, followup_blocks_turns).reshape((QUERIES, KB))
    return {"queries": queries, "passages": passages, "first_blocks": first_blocks, "followup_blocks": followup_blocks}


SOFTMAX_HEAT = 2.0
FEEDBACK = 0.5


def one_group(packed, passages):
    cluster_query_rows, group_first, group_second = packed
    initial_round_rows = passages[group_first]
    match_scores = SOFTMAX_HEAT * jnp.einsum("dt,dbzt->dbz", cluster_query_rows, initial_round_rows, precision=lax.Precision.HIGHEST)
    flat_scores = match_scores.reshape(match_scores.shape[0], -1)
    weights = jax.nn.softmax(flat_scores, axis=1).reshape(match_scores.shape)
    feedback = jnp.einsum("gkr,gkre->ge", weights, initial_round_rows, precision=lax.Precision.HIGHEST)
    expanded = cluster_query_rows + (FEEDBACK * cluster_query_rows.shape[1] ** -0.5) * feedback
    second_rows = passages[group_second]
    second = jnp.einsum("dt,dbzt->dbz", expanded, second_rows, precision=lax.Precision.HIGHEST)
    return expanded, second


def reference(queries, passages, first_blocks, followup_blocks):
    groups = queries.shape[0] // 64
    packed = (queries.reshape(groups, 64, -1), first_blocks.reshape(groups, 64, -1), followup_blocks.reshape(groups, 64, -1))
    expanded, second = lax.map(partial(one_group, passages=passages), packed)
    return expanded.reshape(queries.shape), second.reshape(queries.shape[0], first_blocks.shape[1], -1)
```

```python
import functools

import jax
import jax.numpy as jnp
import numpy as np
from jax import lax
from jax.experimental import pallas as pl
from jax.experimental.pallas import tpu as pltpu
from jax.sharding import PartitionSpec as P

SOFTMAX_HEAT = 2.0
FEEDBACK = 0.5
LOWEST = -3.0e38
NT = (((1,), (1,)), ((), ()))
NN = (((1,), (0,)), ((), ()))


def position_targets(block_ids, capacity):
    flat_ids = block_ids.reshape(-1)
    matches = flat_ids[:, None] == flat_ids[None, :]
    positions = jnp.arange(flat_ids.shape[0], dtype=jnp.int32)
    earlier = positions[None, :] < positions[:, None]
    ranking = jnp.sum(jnp.logical_and(matches, earlier), axis=1, dtype=jnp.int32)
    return flat_ids * capacity + ranking


def pack_rows(values, targets, owners, resident_blocks, capacity):
    buffer = jnp.zeros((owners * resident_blocks * capacity, values.shape[1]), values.dtype)
    buffer = buffer.at[targets].set(values)
    return buffer.reshape(owners, resident_blocks, capacity, values.shape[1])


def reply(results):
    return (
        lax.all_to_all(results[0], "cluster", split_axis=0, concat_axis=0, tiled=True),
        lax.all_to_all(results[1], "cluster", split_axis=0, concat_axis=0, tiled=True),
        lax.all_to_all(results[2], "cluster", split_axis=0, concat_axis=0, tiled=True),
    )


def send_back(match_scores):
    return lax.all_to_all(match_scores, "cluster", split_axis=0, concat_axis=0, tiled=True)


def routed(queries, passages, first_blocks, followup_blocks):
    owners = lax.axis_size("cluster")
    resident_blocks = passages.shape[0]
    embed_width = queries.shape[1]
    per_query = first_blocks.shape[1]
    pair_count = queries.shape[0] * per_query
    all_blocks = owners * resident_blocks
    capacity = max(2, (3 * pair_count + 2 * all_blocks - 1) // (2 * all_blocks))
    coefficient = FEEDBACK * embed_width ** (-0.5)
    highest = lax.Precision.HIGHEST

    def project_onto_centroid(arrived):
        return jnp.einsum("nbce,bre->nbcr", arrived, passages, precision=highest)

    first_targets = position_targets(first_blocks, capacity)
    second_targets = position_targets(followup_blocks, capacity)
    repeated = jnp.repeat(queries, per_query, axis=0)
    first_sent = pack_rows(repeated, first_targets, owners, resident_blocks, capacity)
    match_scores = SOFTMAX_HEAT * project_onto_centroid(
        lax.all_to_all(first_sent, "cluster", split_axis=0, concat_axis=0, tiled=True)
    )
    highs = jnp.max(match_scores, axis=3)
    weights = jnp.exp(match_scores - highs[..., None])
    totals = jnp.sum(weights, axis=3)
    vectors = jnp.einsum("nbcr,bre->nbce", weights, passages, precision=highest)
    highs, totals, vectors = reply((highs, totals, vectors))
    highs = highs.reshape(-1)[first_targets].reshape(-1, per_query)
    totals = totals.reshape(-1)[first_targets].reshape(-1, per_query)
    vectors = vectors.reshape(-1, embed_width)[first_targets].reshape(-1, per_query, embed_width)
    peak_high = jnp.max(highs, axis=1, keepdims=True)
    scaled = jnp.exp(highs - peak_high)
    denominator = jnp.sum(scaled * totals, axis=1)
    feedback = jnp.einsum("qk,qke->qe", scaled, vectors, precision=highest) / denominator[:, None]
    expanded = queries + coefficient * feedback
    expanded_sent = pack_rows(
        jnp.repeat(expanded, per_query, axis=0), second_targets, owners, resident_blocks, capacity
    )
    returned = (lambda arrived: send_back(project_onto_centroid(arrived)))(
        lax.all_to_all(expanded_sent, "cluster", split_axis=0, concat_axis=0, tiled=True)
    )
    second_scores = returned.reshape(-1, returned.shape[3])[second_targets].reshape(
        queries.shape[0], per_query, -1
    )
    return (expanded, second_scores)


class Ladder:
    def __init__(self, where):
        self.where = where
        self.spot = {place: i for i, place in enumerate(where)}

    def hop(self, pairs):
        return [
            (self.spot[a, y, c], self.spot[b, y, c]) for a, b in pairs for y in (0, 1) for c in (0, 1)
        ]

    def across(self, levels=(0, 1, 2, 3)):
        return [
            (i, self.spot[z, 1 - y, c]) for i, (z, y, c) in enumerate(self.where) if z in levels
        ]

    def sibling(self):
        return [(i, self.spot[z, y, 1 - c]) for i, (z, y, c) in enumerate(self.where)]


def ladder_of(mesh):
    groups = np.moveaxis(mesh.devices, mesh.axis_names.index("cluster"), -1)
    groups = groups.reshape(-1, groups.shape[-1])
    found = []
    for group in groups:
        if not all(hasattr(d, "coords") and hasattr(d, "core_on_chip") for d in group):
            return None
        spots = np.array([[*d.coords, d.core_on_chip] for d in group])
        kinds = [np.unique(column) for column in spots.T]
        order = sorted(range(3), key=lambda k: -len(kinds[k]))
        if [len(kinds[k]) for k in order] != [4, 2, 1] or len(kinds[3]) != 2:
            return None
        use = (order[0], order[1], 3)
        found.append([tuple(int(np.searchsorted(kinds[k], s[k])) for k in use) for s in spots])
    if any(f != found[0] for f in found) or len(set(found[0])) != len(found[0]):
        return None
    return Ladder(found[0])


def split(x):
    high = x.astype(jnp.bfloat16)
    return high, (x - high.astype(jnp.float32)).astype(jnp.bfloat16)


def dot(a, b, dims):
    return lax.dot_general(a, b, dims, preferred_element_type=jnp.float32)


def three_way(stacked, high, low, dims):
    rows = stacked.shape[0] // 2
    both = dot(stacked, high, dims)
    return both[:rows] + both[rows:] + dot(stacked[:rows], low, dims)


def stacked_halves(x):
    high, low = split(x)
    return jnp.concatenate([high, low], axis=0)


def first_round(ids, base, picks, slots, inner, queries, named, state, high_ref, low_ref, score_ref):
    rows = slots[0][0].shape[0]
    count = len(slots)
    for k, refs in enumerate(slots):
        block = refs[0][...]
        if len(refs) == 2:
            block = jnp.where(inner, block, refs[1][...])
        high, low = split(block)
        high_ref[k * rows : (k + 1) * rows, :] = high
        low_ref[k * rows : (k + 1) * rows, :] = low
    asked = stacked_halves(queries)
    scores = SOFTMAX_HEAT * three_way(asked, high_ref[...], low_ref[...], NT)
    top = None
    for k in range(count):
        mine = named[0] == ids[base + k]
        for column in named[1:]:
            mine = jnp.logical_or(mine, column == ids[base + k])
        part = jnp.where(mine, scores[:, k * rows : (k + 1) * rows], LOWEST)
        score_ref[:, k * rows : (k + 1) * rows] = part
        top = part if top is None else jnp.maximum(top, part)
    peak, total, vector = state
    new_peak = jnp.maximum(peak, jnp.max(top, axis=1, keepdims=True))
    held = score_ref[...]
    weights = jnp.where(held > LOWEST, jnp.exp(held - new_peak), 0.0)
    scale = jnp.exp(peak - new_peak)
    total = scale * total + jnp.sum(weights, axis=1, keepdims=True)
    gained = three_way(stacked_halves(weights), high_ref[...], low_ref[...], NN)
    return new_peak, total, scale * vector + gained


def columns_of(ref, width):
    return [
        jnp.broadcast_to(ref[:, j : j + 1], (ref.shape[0], width)) for j in range(ref.shape[1])
    ]


def step_kernel(shape, base, fresh, ids, *refs):
    count = len(shape)
    at = 0
    slots = []
    for n in shape:
        slots.append(refs[at : at + n])
        at += n
    q_ref, fb_ref = refs[at : at + 2]
    at += 2
    rows = slots[0][0].shape[0]
    if fresh:
        state = (
            jnp.full((q_ref.shape[0], 1), LOWEST, jnp.float32),
            jnp.zeros((q_ref.shape[0], 1), jnp.float32),
            jnp.zeros(q_ref.shape, jnp.float32),
        )
    else:
        stat, vec = refs[at : at + 2]
        at += 2
        state = (stat[:, 0:1], stat[:, 1:2], vec[...])
    stat_out, vec_out, high_ref, low_ref, score_ref = refs[at:]
    peak, total, vector = first_round(
        ids, base, None, slots, ids[ids.shape[0] - 1] == 1, q_ref[...], columns_of(fb_ref, rows), state,
        high_ref, low_ref, score_ref,
    )
    lane = lax.broadcasted_iota(jnp.int32, stat_out.shape, 1)
    stat_out[...] = jnp.where(lane == 0, peak, total)
    vec_out[...] = vector


def last_kernel(shape, base, held, coefficient, ids, *refs):
    at = 0
    slots = []
    for n in shape:
        slots.append(refs[at : at + n])
        at += n
    q_ref, fb_ref, ub_ref, stat, vec = refs[at : at + 5]
    at += 5
    kept = []
    for start, count in held:
        kept.append((start, count, refs[at], refs[at + 1]))
        at += 2
    expanded_ref, second_ref, high_ref, low_ref, score_ref, named_ref = refs[at:]
    rows = slots[0][0].shape[0]
    kept.append((base, len(shape), high_ref, low_ref))
    queries = q_ref[...]
    peak, total, vector = first_round(
        ids, base, None, slots, ids[ids.shape[0] - 1] == 1, queries, columns_of(fb_ref, rows),
        (stat[:, 0:1], stat[:, 1:2], vec[...]), high_ref, low_ref, score_ref,
    )
    expanded = queries + coefficient * (vector / total)
    expanded_ref[...] = expanded
    asked = stacked_halves(expanded)
    per_query = ub_ref.shape[1]
    for j in range(per_query):
        named_ref[j] = jnp.broadcast_to(ub_ref[:, j : j + 1], (ub_ref.shape[0], rows))
    picked = [jnp.zeros((queries.shape[0], rows), jnp.float32) for _ in range(per_query)]
    for start, count, high, low in kept:
        scores = three_way(asked, high[...], low[...], NT)
        for k in range(count):
            part = scores[:, k * rows : (k + 1) * rows]
            for j in range(per_query):
                picked[j] = jnp.where(named_ref[j] == ids[start + k], part, picked[j])
    for j in range(per_query):
        second_ref[:, j, :] = picked[j]


VMEM = pl.BlockSpec(memory_space=pltpu.VMEM)
SMEM = pl.BlockSpec(memory_space=pltpu.SMEM)


def cost(queries, count, block, rounds):
    flops = 2 * 3 * queries.shape[0] * count * block.shape[0] * block.shape[1] * rounds
    return pl.CostEstimate(
        flops=flops, transcendentals=queries.shape[0] * count * block.shape[0],
        bytes_accessed=4 * count * block.shape[0] * block.shape[1],
    )


def step_call(slots, base, ids, queries, first_blocks, state):
    block = slots[0][0]
    count, rows, width = len(slots), block.shape[0], block.shape[1]
    flat = [ref for slot in slots for ref in slot]
    extra = [] if state is None else list(state)
    many = queries.shape[0]
    return pl.pallas_call(
        functools.partial(step_kernel, tuple(len(s) for s in slots), base, state is None),
        out_shape=(
            jax.ShapeDtypeStruct((many, rows), jnp.float32),
            jax.ShapeDtypeStruct((many, width), jnp.float32),
            jax.ShapeDtypeStruct((count * rows, width), jnp.bfloat16),
            jax.ShapeDtypeStruct((count * rows, width), jnp.bfloat16),
        ),
        in_specs=[SMEM] + [VMEM] * (len(flat) + 2 + len(extra)),
        out_specs=(VMEM,) * 4,
        scratch_shapes=[pltpu.VMEM((many, count * rows), jnp.float32)],
        compiler_params=pltpu.CompilerParams(vmem_limit_bytes=STEP_VMEM),
        cost_estimate=cost(queries, count, block, 2),
        name="first_round_step",
    )(ids, *flat, queries, first_blocks, *extra)


def last_call(slots, base, ids, queries, first_blocks, followup_blocks, state, held):
    block = slots[0][0]
    count, rows, width = len(slots), block.shape[0], block.shape[1]
    flat = [ref for slot in slots for ref in slot]
    many, per_query = followup_blocks.shape
    kept = [a for _, _, high, low in held for a in (high, low)]
    total = count + sum(n for _, n, _, _ in held)
    return pl.pallas_call(
        functools.partial(
            last_kernel, tuple(len(s) for s in slots), base, tuple((s, n) for s, n, _, _ in held),
            FEEDBACK * width ** (-0.5),
        ),
        out_shape=(
            jax.ShapeDtypeStruct((many, width), jnp.float32),
            jax.ShapeDtypeStruct((many, per_query, rows), jnp.float32),
        ),
        in_specs=[SMEM] + [VMEM] * (len(flat) + 5 + len(kept)),
        out_specs=(VMEM,) * 2,
        scratch_shapes=[
            pltpu.VMEM((count * rows, width), jnp.bfloat16),
            pltpu.VMEM((count * rows, width), jnp.bfloat16),
            pltpu.VMEM((many, count * rows), jnp.float32),
            pltpu.VMEM((per_query, many, rows), jnp.int32),
        ],
        compiler_params=pltpu.CompilerParams(vmem_limit_bytes=LAST_VMEM),
        cost_estimate=cost(queries, total, block, 1),
        name="second_round",
    )(ids, *flat, queries, first_blocks, followup_blocks, *state, *kept)


STEP_VMEM = 32 * 2**20
LAST_VMEM = 48 * 2**20


def slot_owner(slot, z, y):
    inner = z in (1, 2)
    other = 1 - y
    return {
        "own": (z, y), "a1": (z ^ 1, y), "a2": (z ^ 2, y), "a3": (z ^ 3, y),
        "y0": (z, other), "y1": (z ^ 3 if inner else z ^ 1, other), "y2": (z ^ 2, other),
        "y3": (z ^ 1 if inner else z ^ 3, other),
    }[slot]


STAGES = (("own", "a1", "y0"), ("a2", "y1"), ("a3", "y2"), ("y3",))


def gathered(ladder, queries, passages, first_blocks, followup_blocks):
    resident = passages.shape[0]
    everywhere = lambda x, pairs: lax.ppermute(x, "cluster", pairs)
    full = ladder.hop([(0, 1), (1, 0), (2, 3), (3, 2)])
    middle = ladder.hop([(1, 2), (2, 1)])
    outward = ladder.hop([(1, 0), (2, 3)])
    inward = ladder.hop([(0, 1), (3, 2)])
    across, across_ends = ladder.across(), ladder.across((0, 3))
    sibling = ladder.sibling()

    table = []
    for z, y, c in ladder.where:
        line = []
        for stage in STAGES:
            for slot in stage:
                for core in (c, 1 - c):
                    owner = ladder.spot[(*slot_owner(slot, z, y), core)]
                    line += [owner * resident + r for r in range(resident)]
        table.append(line + [int(z in (1, 2))])
    me = lax.axis_index("cluster")
    ids = lax.dynamic_slice_in_dim(jnp.asarray(np.array(table, np.int32)), me, 1, 0)[0]
    inner = ids[-1] == 1

    got = {slot: [] for stage in STAGES for slot in stage}
    pieces = []
    for r in range(resident):
        own = passages[r]
        a1 = everywhere(own, full)
        b1 = everywhere(own, middle)
        y0 = everywhere(own, across)
        a2 = jnp.where(inner, everywhere(a1, middle), everywhere(b1, outward))
        a3 = everywhere(a2, outward)
        y1 = everywhere(jnp.where(inner, b1, a1), across)
        d1 = everywhere(y0, inward)
        y2 = everywhere(a2, across)
        last = everywhere(a3, across_ends) if r % 2 == 0 else everywhere(y2, outward)
        pieces.append({
            "own": (own,), "a1": (a1,), "y0": (y0,), "a2": (a2,), "y1": (y1,), "a3": (b1, a3),
            "y2": (y2,), "y3": (d1, last),
        })
    state, held, base = None, [], 0
    for number, stage in enumerate(STAGES):
        slots = []
        for slot in stage:
            slots += [p[slot] for p in pieces]
            slots += [tuple(everywhere(a, sibling) for a in p[slot]) for p in pieces]
        if number + 1 < len(STAGES):
            stat, vector, high, low = step_call(slots, base, ids, queries, first_blocks, state)
            state = (stat, vector)
            held.append((base, len(slots), high, low))
            base += len(slots)
    return last_call(slots, base, ids, queries, first_blocks, followup_blocks, state, held)


def solution(mesh):
    ladder = ladder_of(mesh)

    def local(queries, passages, first_blocks, followup_blocks):
        owners, resident, rows = lax.axis_size("cluster"), *passages.shape[:2]
        pairs, blocks = first_blocks.size, owners * resident
        capacity = max(2, (3 * pairs + 2 * blocks - 1) // (2 * blocks))
        if ladder is not None and blocks * rows <= 2 * 3 * blocks * capacity:
            return gathered(ladder, queries, passages, first_blocks, followup_blocks)
        return routed(queries, passages, first_blocks, followup_blocks)

    return jax.shard_map(
        local,
        mesh=mesh,
        in_specs=(
            P(("parts", "cluster"), None),
            P(("parts", "cluster"), None, None),
            P(("parts", "cluster"), None),
            P(("parts", "cluster"), None),
        ),
        out_specs=(P(("parts", "cluster"), None), P(("parts", "cluster"), None, None)),
        check_vma=False,
    )
```

```python
import functools

import jax
import jax.numpy as jnp
import numpy as np
from jax import lax
from jax.experimental import pallas as pl
from jax.experimental.pallas import tpu as pltpu
from jax.sharding import PartitionSpec as P


SOFTMAX_HEAT = 2.0
FEEDBACK = 0.5
LOWEST = -3.0e38
NT = (((1,), (1,)), ((), ()))
NN = (((1,), (0,)), ((), ()))


def position_targets(block_ids, capacity):
    flat_ids = block_ids.reshape(-1)
    matches = flat_ids[:, None] == flat_ids[None, :]
    positions = jnp.arange(flat_ids.shape[0], dtype=jnp.int32)
    earlier = positions[None, :] < positions[:, None]
    ranking = jnp.sum(jnp.logical_and(matches, earlier), axis=1, dtype=jnp.int32)
    return flat_ids * capacity + ranking


def pack_rows(values, targets, owners, resident_blocks, capacity):
    buffer = jnp.zeros((owners * resident_blocks * capacity, values.shape[1]), values.dtype)
    buffer = buffer.at[targets].set(values)
    return buffer.reshape(owners, resident_blocks, capacity, values.shape[1])


def reply(results):
    return (
        lax.all_to_all(results[0], "cluster", split_axis=0, concat_axis=0, tiled=True),
        lax.all_to_all(results[1], "cluster", split_axis=0, concat_axis=0, tiled=True),
        lax.all_to_all(results[2], "cluster", split_axis=0, concat_axis=0, tiled=True),
    )


def send_back(match_scores):
    return lax.all_to_all(match_scores, "cluster", split_axis=0, concat_axis=0, tiled=True)


def routed(queries, passages, first_blocks, followup_blocks):
    owners = lax.axis_size("cluster")
    resident_blocks = passages.shape[0]
    embed_width = queries.shape[1]
    per_query = first_blocks.shape[1]
    pair_count = queries.shape[0] * per_query
    all_blocks = owners * resident_blocks
    capacity = max(2, (3 * pair_count + 2 * all_blocks - 1) // (2 * all_blocks))
    coefficient = FEEDBACK * embed_width ** (-0.5)
    highest = lax.Precision.HIGHEST

    def project_onto_centroid(arrived):
        return jnp.einsum("nbce,bre->nbcr", arrived, passages, precision=highest)

    first_targets = position_targets(first_blocks, capacity)
    second_targets = position_targets(followup_blocks, capacity)
    repeated = jnp.repeat(queries, per_query, axis=0)
    first_sent = pack_rows(repeated, first_targets, owners, resident_blocks, capacity)
    match_scores = SOFTMAX_HEAT * project_onto_centroid(
        lax.all_to_all(first_sent, "cluster", split_axis=0, concat_axis=0, tiled=True)
    )
    highs = jnp.max(match_scores, axis=3)
    weights = jnp.exp(match_scores - highs[..., None])
    totals = jnp.sum(weights, axis=3)
    vectors = jnp.einsum("nbcr,bre->nbce", weights, passages, precision=highest)
    highs, totals, vectors = reply((highs, totals, vectors))
    highs = highs.reshape(-1)[first_targets].reshape(-1, per_query)
    totals = totals.reshape(-1)[first_targets].reshape(-1, per_query)
    vectors = vectors.reshape(-1, embed_width)[first_targets].reshape(-1, per_query, embed_width)
    peak_high = jnp.max(highs, axis=1, keepdims=True)
    scaled = jnp.exp(highs - peak_high)
    denominator = jnp.sum(scaled * totals, axis=1)
    feedback = jnp.einsum("qk,qke->qe", scaled, vectors, precision=highest) / denominator[:, None]
    expanded = queries + coefficient * feedback
    expanded_sent = pack_rows(
        jnp.repeat(expanded, per_query, axis=0), second_targets, owners, resident_blocks, capacity
    )
    returned = (lambda arrived: send_back(project_onto_centroid(arrived)))(
        lax.all_to_all(expanded_sent, "cluster", split_axis=0, concat_axis=0, tiled=True)
    )
    second_scores = returned.reshape(-1, returned.shape[3])[second_targets].reshape(
        queries.shape[0], per_query, -1
    )
    return (expanded, second_scores)


class Ladder:
    def __init__(self, where):
        self.where = where
        self.spot = {place: i for i, place in enumerate(where)}

    def hop(self, pairs):
        return [
            (self.spot[a, y, c], self.spot[b, y, c]) for a, b in pairs for y in (0, 1) for c in (0, 1)
        ]

    def across(self, levels=(0, 1, 2, 3)):
        return [
            (i, self.spot[z, 1 - y, c]) for i, (z, y, c) in enumerate(self.where) if z in levels
        ]

    def sibling(self):
        return [(i, self.spot[z, y, 1 - c]) for i, (z, y, c) in enumerate(self.where)]


def ladder_of(mesh):
    groups = np.moveaxis(mesh.devices, mesh.axis_names.index("cluster"), -1)
    groups = groups.reshape(-1, groups.shape[-1])
    found = []
    for group in groups:
        if not all(hasattr(d, "coords") and hasattr(d, "core_on_chip") for d in group):
            return None
        spots = np.array([[*d.coords, d.core_on_chip] for d in group])
        kinds = [np.unique(column) for column in spots.T]
        order = sorted(range(3), key=lambda k: -len(kinds[k]))
        if [len(kinds[k]) for k in order] != [4, 2, 1] or len(kinds[3]) != 2:
            return None
        use = (order[0], order[1], 3)
        found.append([tuple(int(np.searchsorted(kinds[k], s[k])) for k in use) for s in spots])
    if any(f != found[0] for f in found) or len(set(found[0])) != len(found[0]):
        return None
    return Ladder(found[0])


def split(x):
    high = x.astype(jnp.bfloat16)
    return high, (x - high.astype(jnp.float32)).astype(jnp.bfloat16)


def dot(a, b, dims):
    return lax.dot_general(a, b, dims, preferred_element_type=jnp.float32)


def three_way(stacked, high, low, dims):
    rows = stacked.shape[0] // 2
    both = dot(stacked, high, dims)
    return both[:rows] + both[rows:] + dot(stacked[:rows], low, dims)


def stacked_halves(x):
    high, low = split(x)
    return jnp.concatenate([high, low], axis=0)


def first_round(ids, base, slots, inner, queries, named, state, high_ref, low_ref, score_ref):
    rows = slots[0][0].shape[0]
    count = len(slots)
    for k, refs in enumerate(slots):
        block = refs[0][...]
        if len(refs) == 2:
            block = jnp.where(inner, block, refs[1][...])
        high, low = split(block)
        high_ref[k * rows : (k + 1) * rows, :] = high
        low_ref[k * rows : (k + 1) * rows, :] = low
    asked = stacked_halves(queries)
    scores = SOFTMAX_HEAT * three_way(asked, high_ref[...], low_ref[...], NT)
    top = None
    for k in range(count):
        mine = named[0] == ids[base + k]
        for column in named[1:]:
            mine = jnp.logical_or(mine, column == ids[base + k])
        part = jnp.where(mine, scores[:, k * rows : (k + 1) * rows], LOWEST)
        score_ref[:, k * rows : (k + 1) * rows] = part
        top = part if top is None else jnp.maximum(top, part)
    peak, total, vector = state
    new_peak = jnp.maximum(peak, jnp.max(top, axis=1, keepdims=True))
    held = score_ref[...]
    weights = jnp.where(held > LOWEST, jnp.exp(held - new_peak), 0.0)
    scale = jnp.exp(peak - new_peak)
    total = scale * total + jnp.sum(weights, axis=1, keepdims=True)
    gained = three_way(stacked_halves(weights), high_ref[...], low_ref[...], NN)
    return new_peak, total, scale * vector + gained


def columns_of(ref, width):
    return [
        jnp.broadcast_to(ref[:, j : j + 1], (ref.shape[0], width)) for j in range(ref.shape[1])
    ]


def step_kernel(shape, base, fresh, ids, *refs):
    at = 0
    slots = []
    for n in shape:
        slots.append(refs[at : at + n])
        at += n
    q_ref, fb_ref = refs[at : at + 2]
    at += 2
    rows = slots[0][0].shape[0]
    if fresh:
        state = (
            jnp.full((q_ref.shape[0], 1), LOWEST, jnp.float32),
            jnp.zeros((q_ref.shape[0], 1), jnp.float32),
            jnp.zeros(q_ref.shape, jnp.float32),
        )
    else:
        stat, vec = refs[at : at + 2]
        at += 2
        state = (stat[:, 0:1], stat[:, 1:2], vec[...])
    stat_out, vec_out, high_ref, low_ref, score_ref = refs[at:]
    peak, total, vector = first_round(
        ids, base, slots, ids[ids.shape[0] - 1] == 1, q_ref[...], columns_of(fb_ref, rows), state,
        high_ref, low_ref, score_ref,
    )
    lane = lax.broadcasted_iota(jnp.int32, stat_out.shape, 1)
    stat_out[...] = jnp.where(lane == 0, peak, total)
    vec_out[...] = vector


def last_kernel(shape, base, held, coefficient, ids, *refs):
    at = 0
    slots = []
    for n in shape:
        slots.append(refs[at : at + n])
        at += n
    q_ref, fb_ref, ub_ref, stat, vec = refs[at : at + 5]
    at += 5
    kept = []
    for start, count in held:
        kept.append((start, count, refs[at], refs[at + 1]))
        at += 2
    expanded_ref, second_ref, high_ref, low_ref, score_ref, named_ref = refs[at:]
    rows = slots[0][0].shape[0]
    kept.append((base, len(shape), high_ref, low_ref))
    queries = q_ref[...]
    _, total, vector = first_round(
        ids, base, slots, ids[ids.shape[0] - 1] == 1, queries, columns_of(fb_ref, rows),
        (stat[:, 0:1], stat[:, 1:2], vec[...]), high_ref, low_ref, score_ref,
    )
    expanded = queries + coefficient * (vector / total)
    expanded_ref[...] = expanded
    asked = stacked_halves(expanded)
    per_query = ub_ref.shape[1]
    for j in range(per_query):
        named_ref[j] = jnp.broadcast_to(ub_ref[:, j : j + 1], (ub_ref.shape[0], rows))
    picked = [jnp.zeros((queries.shape[0], rows), jnp.float32) for _ in range(per_query)]
    for start, count, high, low in kept:
        scores = three_way(asked, high[...], low[...], NT)
        for k in range(count):
            part = scores[:, k * rows : (k + 1) * rows]
            for j in range(per_query):
                picked[j] = jnp.where(named_ref[j] == ids[start + k], part, picked[j])
    for j in range(per_query):
        second_ref[:, j, :] = picked[j]


VMEM = pl.BlockSpec(memory_space=pltpu.VMEM)
SMEM = pl.BlockSpec(memory_space=pltpu.SMEM)


def cost(queries, count, block, rounds):
    flops = 2 * 3 * queries.shape[0] * count * block.shape[0] * block.shape[1] * rounds
    return pl.CostEstimate(
        flops=flops, transcendentals=queries.shape[0] * count * block.shape[0],
        bytes_accessed=4 * count * block.shape[0] * block.shape[1],
    )


def step_call(slots, base, ids, queries, first_blocks, state):
    block = slots[0][0]
    count, rows, width = len(slots), block.shape[0], block.shape[1]
    flat = [ref for slot in slots for ref in slot]
    extra = [] if state is None else list(state)
    many = queries.shape[0]
    return pl.pallas_call(
        functools.partial(step_kernel, tuple(len(s) for s in slots), base, state is None),
        out_shape=(
            jax.ShapeDtypeStruct((many, rows), jnp.float32),
            jax.ShapeDtypeStruct((many, width), jnp.float32),
            jax.ShapeDtypeStruct((count * rows, width), jnp.bfloat16),
            jax.ShapeDtypeStruct((count * rows, width), jnp.bfloat16),
        ),
        in_specs=[SMEM] + [VMEM] * (len(flat) + 2 + len(extra)),
        out_specs=(VMEM,) * 4,
        scratch_shapes=[pltpu.VMEM((many, count * rows), jnp.float32)],
        compiler_params=pltpu.CompilerParams(vmem_limit_bytes=STEP_VMEM),
        cost_estimate=cost(queries, count, block, 2),
        name="first_round_step",
    )(ids, *flat, queries, first_blocks, *extra)


def last_call(slots, base, ids, queries, first_blocks, followup_blocks, state, held):
    block = slots[0][0]
    count, rows, width = len(slots), block.shape[0], block.shape[1]
    flat = [ref for slot in slots for ref in slot]
    many, per_query = followup_blocks.shape
    kept = [a for _, _, high, low in held for a in (high, low)]
    total = count + sum(n for _, n, _, _ in held)
    return pl.pallas_call(
        functools.partial(
            last_kernel, tuple(len(s) for s in slots), base, tuple((s, n) for s, n, _, _ in held),
            FEEDBACK * width ** (-0.5),
        ),
        out_shape=(
            jax.ShapeDtypeStruct((many, width), jnp.float32),
            jax.ShapeDtypeStruct((many, per_query, rows), jnp.float32),
        ),
        in_specs=[SMEM] + [VMEM] * (len(flat) + 5 + len(kept)),
        out_specs=(VMEM,) * 2,
        scratch_shapes=[
            pltpu.VMEM((count * rows, width), jnp.bfloat16),
            pltpu.VMEM((count * rows, width), jnp.bfloat16),
            pltpu.VMEM((many, count * rows), jnp.float32),
            pltpu.VMEM((per_query, many, rows), jnp.int32),
        ],
        compiler_params=pltpu.CompilerParams(vmem_limit_bytes=LAST_VMEM),
        cost_estimate=cost(queries, total, block, 1),
        name="second_round",
    )(ids, *flat, queries, first_blocks, followup_blocks, *state, *kept)


STEP_VMEM = 12 * 2**20
LAST_VMEM = 12 * 2**20


def slot_owner(slot, z, y):
    inner = z in (1, 2)
    other = 1 - y
    return {
        "own": (z, y), "a1": (z ^ 1, y), "a2": (z ^ 2, y), "a3": (z ^ 3, y),
        "y0": (z, other), "y1": (z ^ 3 if inner else z ^ 1, other), "y2": (z ^ 2, other),
        "y3": (z ^ 1 if inner else z ^ 3, other),
    }[slot]


STAGES = (("own", "a1", "y0"), ("a2", "y1"), ("a3", "y2"), ("y3",))


def gathered(ladder, queries, passages, first_blocks, followup_blocks):
    resident = passages.shape[0]

    def send(x, pairs):
        return lax.ppermute(x, "cluster", pairs)

    full = ladder.hop([(0, 1), (1, 0), (2, 3), (3, 2)])
    middle = ladder.hop([(1, 2), (2, 1)])
    outward = ladder.hop([(1, 0), (2, 3)])
    inward = ladder.hop([(0, 1), (3, 2)])
    across, across_ends = ladder.across(), ladder.across((0, 3))
    sibling = ladder.sibling()

    table = []
    for z, y, c in ladder.where:
        line = []
        for stage in STAGES:
            for slot in stage:
                for core in (c, 1 - c):
                    owner = ladder.spot[(*slot_owner(slot, z, y), core)]
                    line += [owner * resident + r for r in range(resident)]
        table.append(line + [int(z in (1, 2))])
    me = lax.axis_index("cluster")
    ids = lax.dynamic_slice_in_dim(jnp.asarray(np.array(table, np.int32)), me, 1, 0)[0]
    inner = ids[-1] == 1

    pieces = []
    for r in range(resident):
        own = passages[r]
        a1 = send(own, full)
        b1 = send(own, middle)
        y0 = send(own, across)
        a2 = jnp.where(inner, send(a1, middle), send(b1, outward))
        a3 = send(a2, outward)
        y1 = send(jnp.where(inner, b1, a1), across)
        d1 = send(y0, inward)
        y2 = send(a2, across)
        last = send(a3, across_ends) if r % 2 == 0 else send(y2, outward)
        pieces.append({
            "own": (own,), "a1": (a1,), "y0": (y0,), "a2": (a2,), "y1": (y1,), "a3": (b1, a3),
            "y2": (y2,), "y3": (d1, last),
        })
    state, held, base = None, [], 0
    for number, stage in enumerate(STAGES):
        slots = []
        for slot in stage:
            slots += [p[slot] for p in pieces]
            slots += [tuple(send(a, sibling) for a in p[slot]) for p in pieces]
        if number + 1 < len(STAGES):
            stat, vector, high, low = step_call(slots, base, ids, queries, first_blocks, state)
            state = (stat, vector)
            held.append((base, len(slots), high, low))
            base += len(slots)
    return last_call(slots, base, ids, queries, first_blocks, followup_blocks, state, held)


def solution(mesh):
    ladder = ladder_of(mesh)

    def local(queries, passages, first_blocks, followup_blocks):
        owners, resident, rows = lax.axis_size("cluster"), *passages.shape[:2]
        pairs, blocks = first_blocks.size, owners * resident
        capacity = max(2, (3 * pairs + 2 * blocks - 1) // (2 * blocks))
        if ladder is not None and blocks * rows <= 2 * 3 * blocks * capacity:
            return gathered(ladder, queries, passages, first_blocks, followup_blocks)
        return routed(queries, passages, first_blocks, followup_blocks)

    return jax.shard_map(
        local,
        mesh=mesh,
        in_specs=(
            P(("parts", "cluster"), None),
            P(("parts", "cluster"), None, None),
            P(("parts", "cluster"), None),
            P(("parts", "cluster"), None),
        ),
        out_specs=(P(("parts", "cluster"), None), P(("parts", "cluster"), None, None)),
        check_vma=False,
    )
```

```python
import functools

import jax
import jax.numpy as jnp
import numpy as np
from jax import lax
from jax.experimental import pallas as pl
from jax.experimental.pallas import tpu as pltpu
from jax.sharding import PartitionSpec as P


SOFTMAX_HEAT = 2.0
FEEDBACK = 0.5
LOWEST = -3.0e38
NT = (((1,), (1,)), ((), ()))
NN = (((1,), (0,)), ((), ()))


def position_targets(block_ids, capacity):
    flat_ids = block_ids.reshape(-1)
    matches = flat_ids[:, None] == flat_ids[None, :]
    positions = jnp.arange(flat_ids.shape[0], dtype=jnp.int32)
    earlier = positions[None, :] < positions[:, None]
    ranking = jnp.sum(jnp.logical_and(matches, earlier), axis=1, dtype=jnp.int32)
    return flat_ids * capacity + ranking


def pack_rows(values, targets, owners, resident_blocks, capacity):
    buffer = jnp.zeros((owners * resident_blocks * capacity, values.shape[1]), values.dtype)
    buffer = buffer.at[targets].set(values)
    return buffer.reshape(owners, resident_blocks, capacity, values.shape[1])


def reply(results):
    return (
        lax.all_to_all(results[0], "cluster", split_axis=0, concat_axis=0, tiled=True),
        lax.all_to_all(results[1], "cluster", split_axis=0, concat_axis=0, tiled=True),
        lax.all_to_all(results[2], "cluster", split_axis=0, concat_axis=0, tiled=True),
    )


def send_back(match_scores):
    return lax.all_to_all(match_scores, "cluster", split_axis=0, concat_axis=0, tiled=True)


def routed(queries, passages, first_blocks, followup_blocks):
    owners = lax.axis_size("cluster")
    resident_blocks = passages.shape[0]
    embed_width = queries.shape[1]
    per_query = first_blocks.shape[1]
    pair_count = queries.shape[0] * per_query
    all_blocks = owners * resident_blocks
    capacity = max(2, (3 * pair_count + 2 * all_blocks - 1) // (2 * all_blocks))
    coefficient = FEEDBACK * embed_width ** (-0.5)
    highest = lax.Precision.HIGHEST

    def project_onto_centroid(arrived):
        return jnp.einsum("nbce,bre->nbcr", arrived, passages, precision=highest)

    first_targets = position_targets(first_blocks, capacity)
    second_targets = position_targets(followup_blocks, capacity)
    repeated = jnp.repeat(queries, per_query, axis=0)
    first_sent = pack_rows(repeated, first_targets, owners, resident_blocks, capacity)
    match_scores = SOFTMAX_HEAT * project_onto_centroid(
        lax.all_to_all(first_sent, "cluster", split_axis=0, concat_axis=0, tiled=True)
    )
    highs = jnp.max(match_scores, axis=3)
    weights = jnp.exp(match_scores - highs[..., None])
    totals = jnp.sum(weights, axis=3)
    vectors = jnp.einsum("nbcr,bre->nbce", weights, passages, precision=highest)
    highs, totals, vectors = reply((highs, totals, vectors))
    highs = highs.reshape(-1)[first_targets].reshape(-1, per_query)
    totals = totals.reshape(-1)[first_targets].reshape(-1, per_query)
    vectors = vectors.reshape(-1, embed_width)[first_targets].reshape(-1, per_query, embed_width)
    peak_high = jnp.max(highs, axis=1, keepdims=True)
    scaled = jnp.exp(highs - peak_high)
    denominator = jnp.sum(scaled * totals, axis=1)
    feedback = jnp.einsum("qk,qke->qe", scaled, vectors, precision=highest) / denominator[:, None]
    expanded = queries + coefficient * feedback
    expanded_sent = pack_rows(
        jnp.repeat(expanded, per_query, axis=0), second_targets, owners, resident_blocks, capacity
    )
    returned = (lambda arrived: send_back(project_onto_centroid(arrived)))(
        lax.all_to_all(expanded_sent, "cluster", split_axis=0, concat_axis=0, tiled=True)
    )
    second_scores = returned.reshape(-1, returned.shape[3])[second_targets].reshape(
        queries.shape[0], per_query, -1
    )
    return (expanded, second_scores)


class Ladder:
    def __init__(self, where):
        self.where = where
        self.spot = {place: i for i, place in enumerate(where)}

    def hop(self, pairs):
        return [
            (self.spot[a, y, c], self.spot[b, y, c]) for a, b in pairs for y in (0, 1) for c in (0, 1)
        ]

    def across(self, levels=(0, 1, 2, 3)):
        return [
            (i, self.spot[z, 1 - y, c]) for i, (z, y, c) in enumerate(self.where) if z in levels
        ]

    def sibling(self):
        return [(i, self.spot[z, y, 1 - c]) for i, (z, y, c) in enumerate(self.where)]


def ladder_of(mesh):
    groups = np.moveaxis(mesh.devices, mesh.axis_names.index("cluster"), -1)
    groups = groups.reshape(-1, groups.shape[-1])
    found = []
    for group in groups:
        if not all(hasattr(d, "coords") and hasattr(d, "core_on_chip") for d in group):
            return None
        spots = np.array([[*d.coords, d.core_on_chip] for d in group])
        kinds = [np.unique(column) for column in spots.T]
        order = sorted(range(3), key=lambda k: -len(kinds[k]))
        if [len(kinds[k]) for k in order] != [4, 2, 1] or len(kinds[3]) != 2:
            return None
        use = (order[0], order[1], 3)
        found.append([tuple(int(np.searchsorted(kinds[k], s[k])) for k in use) for s in spots])
    if any(f != found[0] for f in found) or len(set(found[0])) != len(found[0]):
        return None
    return Ladder(found[0])


def split(x):
    high = x.astype(jnp.bfloat16)
    return high, (x - high.astype(jnp.float32)).astype(jnp.bfloat16)


def dot(a, b, dims):
    return lax.dot_general(a, b, dims, preferred_element_type=jnp.float32)


def three_way(stacked, high, low, dims):
    rows = stacked.shape[0] // 2
    both = dot(stacked, high, dims)
    return both[:rows] + both[rows:] + dot(stacked[:rows], low, dims)


def stacked_halves(x):
    high, low = split(x)
    return jnp.concatenate([high, low], axis=0)


def first_round(ids, base, slots, inner, queries, named, state, high_ref, low_ref, score_ref):
    rows = slots[0][0].shape[0]
    count = len(slots)
    for k, refs in enumerate(slots):
        block = refs[0][...]
        if len(refs) == 2:
            block = jnp.where(inner, block, refs[1][...])
        high, low = split(block)
        high_ref[k * rows : (k + 1) * rows, :] = high
        low_ref[k * rows : (k + 1) * rows, :] = low
    asked = stacked_halves(queries)
    scores = SOFTMAX_HEAT * three_way(asked, high_ref[...], low_ref[...], NT)
    top = None
    for k in range(count):
        mine = named[0] == ids[base + k]
        for column in named[1:]:
            mine = jnp.logical_or(mine, column == ids[base + k])
        part = jnp.where(mine, scores[:, k * rows : (k + 1) * rows], LOWEST)
        score_ref[:, k * rows : (k + 1) * rows] = part
        top = part if top is None else jnp.maximum(top, part)
    peak, total, vector = state
    new_peak = jnp.maximum(peak, jnp.max(top, axis=1, keepdims=True))
    held = score_ref[...]
    weights = jnp.where(held > LOWEST, jnp.exp(held - new_peak), 0.0)
    scale = jnp.exp(peak - new_peak)
    total = scale * total + jnp.sum(weights, axis=1, keepdims=True)
    gained = three_way(stacked_halves(weights), high_ref[...], low_ref[...], NN)
    return new_peak, total, scale * vector + gained


def columns_of(ref, width):
    return [
        jnp.broadcast_to(ref[j : j + 1, :], (width, ref.shape[1])).T for j in range(ref.shape[0])
    ]


def step_kernel(shape, base, fresh, ids, *refs):
    at = 0
    slots = []
    for n in shape:
        slots.append(refs[at : at + n])
        at += n
    q_ref, fb_ref = refs[at : at + 2]
    at += 2
    rows = slots[0][0].shape[0]
    if fresh:
        state = (
            jnp.full((q_ref.shape[0], 1), LOWEST, jnp.float32),
            jnp.zeros((q_ref.shape[0], 1), jnp.float32),
            jnp.zeros(q_ref.shape, jnp.float32),
        )
    else:
        stat, vec = refs[at : at + 2]
        at += 2
        state = (stat[:, 0:1], stat[:, 1:2], vec[...])
    stat_out, vec_out, high_ref, low_ref, score_ref = refs[at:]
    peak, total, vector = first_round(
        ids, base, slots, ids[ids.shape[0] - 1] == 1, q_ref[...], columns_of(fb_ref, rows), state,
        high_ref, low_ref, score_ref,
    )
    lane = lax.broadcasted_iota(jnp.int32, stat_out.shape, 1)
    stat_out[...] = jnp.where(lane == 0, peak, total)
    vec_out[...] = vector


def last_kernel(shape, base, held, coefficient, ids, *refs):
    at = 0
    slots = []
    for n in shape:
        slots.append(refs[at : at + n])
        at += n
    q_ref, fb_ref, ub_ref, stat, vec = refs[at : at + 5]
    at += 5
    kept = []
    for start, count in held:
        kept.append((start, count, refs[at], refs[at + 1]))
        at += 2
    expanded_ref, second_ref, high_ref, low_ref, score_ref, named_ref = refs[at:]
    rows = slots[0][0].shape[0]
    kept.append((base, len(shape), high_ref, low_ref))
    queries = q_ref[...]
    _, total, vector = first_round(
        ids, base, slots, ids[ids.shape[0] - 1] == 1, queries, columns_of(fb_ref, rows),
        (stat[:, 0:1], stat[:, 1:2], vec[...]), high_ref, low_ref, score_ref,
    )
    expanded = queries + coefficient * (vector / total)
    expanded_ref[...] = expanded
    asked = stacked_halves(expanded)
    per_query = ub_ref.shape[0]
    for j, column in enumerate(columns_of(ub_ref, rows)):
        named_ref[j] = column
    picked = [jnp.zeros((queries.shape[0], rows), jnp.float32) for _ in range(per_query)]
    for start, count, high, low in kept:
        scores = three_way(asked, high[...], low[...], NT)
        for k in range(count):
            part = scores[:, k * rows : (k + 1) * rows]
            for j in range(per_query):
                picked[j] = jnp.where(named_ref[j] == ids[start + k], part, picked[j])
    for j in range(per_query):
        second_ref[:, j, :] = picked[j]


VMEM = pl.BlockSpec(memory_space=pltpu.VMEM)
SMEM = pl.BlockSpec(memory_space=pltpu.SMEM)


def cost(queries, count, block, rounds):
    flops = 2 * 3 * queries.shape[0] * count * block.shape[0] * block.shape[1] * rounds
    return pl.CostEstimate(
        flops=flops, transcendentals=queries.shape[0] * count * block.shape[0],
        bytes_accessed=4 * count * block.shape[0] * block.shape[1],
    )


def step_call(slots, base, ids, queries, first_blocks, state):
    block = slots[0][0]
    count, rows, width = len(slots), block.shape[0], block.shape[1]
    flat = [ref for slot in slots for ref in slot]
    extra = [] if state is None else list(state)
    many = queries.shape[0]
    return pl.pallas_call(
        functools.partial(step_kernel, tuple(len(s) for s in slots), base, state is None),
        out_shape=(
            jax.ShapeDtypeStruct((many, rows), jnp.float32),
            jax.ShapeDtypeStruct((many, width), jnp.float32),
            jax.ShapeDtypeStruct((count * rows, width), jnp.bfloat16),
            jax.ShapeDtypeStruct((count * rows, width), jnp.bfloat16),
        ),
        in_specs=[SMEM] + [VMEM] * (len(flat) + 2 + len(extra)),
        out_specs=(VMEM,) * 4,
        scratch_shapes=[pltpu.VMEM((many, count * rows), jnp.float32)],
        compiler_params=pltpu.CompilerParams(vmem_limit_bytes=STEP_VMEM),
        cost_estimate=cost(queries, count, block, 2),
        name="first_round_step",
    )(ids, *flat, queries, first_blocks, *extra)


def last_call(slots, base, ids, queries, first_blocks, followup_blocks, state, held):
    block = slots[0][0]
    count, rows, width = len(slots), block.shape[0], block.shape[1]
    flat = [ref for slot in slots for ref in slot]
    per_query, many = followup_blocks.shape
    kept = [a for _, _, high, low in held for a in (high, low)]
    total = count + sum(n for _, n, _, _ in held)
    return pl.pallas_call(
        functools.partial(
            last_kernel, tuple(len(s) for s in slots), base, tuple((s, n) for s, n, _, _ in held),
            FEEDBACK * width ** (-0.5),
        ),
        out_shape=(
            jax.ShapeDtypeStruct((many, width), jnp.float32),
            jax.ShapeDtypeStruct((many, per_query, rows), jnp.float32),
        ),
        in_specs=[SMEM] + [VMEM] * (len(flat) + 5 + len(kept)),
        out_specs=(VMEM,) * 2,
        scratch_shapes=[
            pltpu.VMEM((count * rows, width), jnp.bfloat16),
            pltpu.VMEM((count * rows, width), jnp.bfloat16),
            pltpu.VMEM((many, count * rows), jnp.float32),
            pltpu.VMEM((per_query, many, rows), jnp.int32),
        ],
        compiler_params=pltpu.CompilerParams(vmem_limit_bytes=LAST_VMEM),
        cost_estimate=cost(queries, total, block, 1),
        name="second_round",
    )(ids, *flat, queries, first_blocks, followup_blocks, *state, *kept)


STEP_VMEM = 12 * 2**20
LAST_VMEM = 12 * 2**20


def slot_owner(slot, z, y):
    inner = z in (1, 2)
    other = 1 - y
    return {
        "own": (z, y), "a1": (z ^ 1, y), "a2": (z ^ 2, y), "a3": (z ^ 3, y),
        "y0": (z, other), "y1": (z ^ 3 if inner else z ^ 1, other), "y2": (z ^ 2, other),
        "y3": (z ^ 1 if inner else z ^ 3, other),
    }[slot]


STAGES = (("own", "a1", "y0"), ("a2", "y1"), ("a3", "y2"), ("y3",))


def gathered(ladder, queries, passages, first_blocks, followup_blocks):
    resident = passages.shape[0]

    def send(x, pairs):
        return lax.ppermute(x, "cluster", pairs)

    full = ladder.hop([(0, 1), (1, 0), (2, 3), (3, 2)])
    middle = ladder.hop([(1, 2), (2, 1)])
    outward = ladder.hop([(1, 0), (2, 3)])
    inward = ladder.hop([(0, 1), (3, 2)])
    across, across_ends = ladder.across(), ladder.across((0, 3))
    sibling = ladder.sibling()

    table = []
    for z, y, c in ladder.where:
        line = []
        for stage in STAGES:
            for slot in stage:
                for core in (c, 1 - c):
                    owner = ladder.spot[(*slot_owner(slot, z, y), core)]
                    line += [owner * resident + r for r in range(resident)]
        table.append(line + [int(z in (1, 2))])
    me = lax.axis_index("cluster")
    ids = lax.dynamic_slice_in_dim(jnp.asarray(np.array(table, np.int32)), me, 1, 0)[0]
    inner = ids[-1] == 1

    pieces = []
    for r in range(resident):
        own = passages[r]
        a1 = send(own, full)
        b1 = send(own, middle)
        y0 = send(own, across)
        a2 = jnp.where(inner, send(a1, middle), send(b1, outward))
        a3 = send(a2, outward)
        y1 = send(jnp.where(inner, b1, a1), across)
        d1 = send(y0, inward)
        y2 = send(a2, across)
        last = send(a3, across_ends) if r % 2 == 0 else send(y2, outward)
        pieces.append({
            "own": (own,), "a1": (a1,), "y0": (y0,), "a2": (a2,), "y1": (y1,), "a3": (b1, a3),
            "y2": (y2,), "y3": (d1, last),
        })
    state, held, base = None, [], 0
    for number, stage in enumerate(STAGES):
        slots = []
        for slot in stage:
            slots += [p[slot] for p in pieces]
            slots += [tuple(send(a, sibling) for a in p[slot]) for p in pieces]
        if number + 1 < len(STAGES):
            stat, vector, high, low = step_call(slots, base, ids, queries, first_blocks, state)
            state = (stat, vector)
            held.append((base, len(slots), high, low))
            base += len(slots)
    return last_call(slots, base, ids, queries, first_blocks, followup_blocks, state, held)


def solution(mesh):
    ladder = ladder_of(mesh)

    def local(queries, passages, first_blocks, followup_blocks):
        owners, resident, rows = lax.axis_size("cluster"), *passages.shape[:2]
        pairs, blocks = first_blocks.size, owners * resident
        capacity = max(2, (3 * pairs + 2 * blocks - 1) // (2 * blocks))
        if ladder is not None and blocks * rows <= 2 * 3 * blocks * capacity:
            return gathered(ladder, queries, passages, first_blocks.T, followup_blocks.T)
        return routed(queries, passages, first_blocks, followup_blocks)

    return jax.shard_map(
        local,
        mesh=mesh,
        in_specs=(
            P(("parts", "cluster"), None),
            P(("parts", "cluster"), None, None),
            P(("parts", "cluster"), None),
            P(("parts", "cluster"), None),
        ),
        out_specs=(P(("parts", "cluster"), None), P(("parts", "cluster"), None, None)),
        check_vma=False,
    )
```
